32 devices in a mesh: outer: 2 (over x), inner: 16 (over z, y, core).
Axes of the slice: x: 2, y: 2, z: 4, core: 2. Of those that a mesh axis runs over, the one named last changes fastest.
Arguments:
- points: bfloat16 [16, 131072], P(None, ('outer', 'inner')), may hold values from -3 to 3
- charges: bfloat16 [64, 131072], P(None, ('outer', 'inner')), may hold values from -6 to 6
- near_leaves: int32 [512, 16], P(('outer', 'inner')), may hold values from 0 to 511, as said below
- skel_device: int32 [32, 512], P(('outer', 'inner')), may hold values from 0 to 4095, as said below
- skel_tree: int32 [32, 4, 512], P(('outer', 'inner')), may hold values from 0 to 1023, as said below
Outputs:
- potential: float32 [64, 131072], P(None, ('outer', 'inner'))
The draws below stay inside these ranges and needn't reach their ends.
Inputs may be any that keep to these rules, and one draw needn't show every extreme that they name: `near_leaves`: row b holds 16 different leaf numbers, b among them, each a leaf of b's level-0 node or of the level-0 nodes just before and just after it. `skel_device`: row c holds 512 different offsets among the 4096 points of level-0 node c. skel_tree[c, k] holds 512 different positions among the 1024 skeleton points of the children of the level-(k+1) node that contains level-0 node c; all level-0 nodes inside one level-(k+1) node have equal rows k.
All inputs are finite; a program needn't handle non-finite values.
Results may differ from the reference program's by a relative error of at most 0.0035.
Values may be sent and summed in bfloat16 or wider, within the bound.
A program may use at most 64 MiB of HBM per device.

```python
import jax
import jax.numpy as jnp
from jax import lax

DIM = 16
NRHS = 64
LEAF = 256
R = 512
NNEAR = 16
LEAF_DEV = 16
NODES = 32
NDEV = 4096
NLEAVES = 512
NPTS = 131072
LEVELS = 5


def draw_points(key, part):

    def unit_terms(salt, count):
        sub_key = jax.random.fold_in(key, salt)
        return jnp.clip(jax.random.normal(sub_key, (DIM, count), jnp.float32), -4.0, 4.0)
    total = 0.53 * unit_terms(1, NPTS)
    total = total + 0.32 * jnp.repeat(unit_terms(2, NLEAVES), LEAF, axis=1)
    for height in range(LEVELS):
        groups = NODES >> height
        factor = 0.6 if height == 0 else 0.38
        total = total + factor * jnp.repeat(unit_terms(3 + height, groups), NPTS // groups, axis=1)
    return jnp.clip(total, -3.0, 3.0).astype(jnp.bfloat16)


def draw_near_leaves(key, part):
    window = 3 * LEAF_DEV
    leaf_ids = jnp.arange(NLEAVES, dtype=jnp.int32)
    offsets = jnp.arange(window, dtype=jnp.int32)
    first = (leaf_ids // LEAF_DEV - 1) * LEAF_DEV
    candidate = first[:, None] + offsets[None, :]
    inside = (candidate >= 0) & (candidate < NLEAVES)
    scores = jax.random.randint(key, (NLEAVES, window), 0, 2 ** 20, dtype=jnp.int32) * window + offsets[None, :]
    scores = jnp.where(candidate == leaf_ids[:, None], 2 ** 30, scores)
    scores = jnp.where(inside, scores, -1)
    ranked, picked = lax.top_k(scores, NNEAR)
    return jnp.take_along_axis(candidate, picked, axis=1).astype(jnp.int32)


def draw_skel_device(key, part):

    def one_node(node_id):
        return jax.random.permutation(jax.random.fold_in(key, node_id), NDEV)[:R]
    return jax.vmap(one_node)(jnp.arange(NODES, dtype=jnp.int32)).astype(jnp.int32)


def draw_skel_tree(key, part):
    base_key = jax.random.fold_in(key, 91)
    layers = []
    for height in range(LEVELS - 1):
        groups = NODES >> height + 1
        layer_key = jax.random.fold_in(base_key, height)

        def one_group(group_id):
            return jax.random.permutation(jax.random.fold_in(layer_key, group_id), 2 * R)[:R]
        chosen = jax.vmap(one_group)(jnp.arange(groups, dtype=jnp.int32))
        layers.append(jnp.repeat(chosen, 2 ** (height + 1), axis=0))
    return jnp.stack(layers, axis=1).astype(jnp.int32)


def block_levels(own_key, extent, split, low, largest):
    def one(position, blocks):
        draws = jax.random.uniform(jax.random.fold_in(jax.random.fold_in(own_key, 6), position), (blocks,), jnp.float32, low / len(split), largest / len(split))
        return jnp.repeat(jnp.exp(draws), extent[position] // blocks).reshape((-1,) + (1,) * (len(extent) - position - 1))

    loudness = one(*split[0])
    for cut in split[1:]:
        loudness = loudness * one(*cut)
    return loudness


def normal_values(own_key, dims, deviation, reach, cuts=(), held_as=jnp.bfloat16):
    drawn = jax.random.normal(own_key, dims, jnp.float32) * deviation
    if len(cuts) > 0:
        drawn = block_levels(own_key, dims, cuts, -0.22, 0.18) * drawn
    return jnp.clip(drawn, min=-reach, max=reach).astype(held_as)


def setup_inputs(seed: int = 0) -> dict:
    splits = jax.random.split(jax.random.key(seed), 6)
    return {
        "points": draw_points(jax.random.fold_in(splits[5], 71), 0),
        "charges": normal_values(splits[1], (NRHS, NPTS), 1.0, 6.0, ((1, 32),)),
        "near_leaves": draw_near_leaves(jax.random.fold_in(splits[5], 71), 0),
        "skel_device": draw_skel_device(jax.random.fold_in(splits[5], 71), 0),
        "skel_tree": draw_skel_tree(jax.random.fold_in(splits[5], 71), 0),
    }


GAMMA = 0.125


def kernel_block(left, right):
    left32 = left.astype(jnp.float32)
    right32 = right.astype(jnp.float32)
    products = jnp.einsum("dm,dn->mn", left32, right32, precision=lax.Precision.HIGHEST)
    distance = jnp.sum(left32 * left32, 0)[:, None] + jnp.sum(right32 * right32, 0)[None, :] - 2.0 * products
    return jnp.exp(-GAMMA * distance).astype(jnp.bfloat16)


def spread_weights(weights, block):
    totals = jnp.sum(block.astype(jnp.float32), 1)
    return (weights.astype(jnp.float32) / totals[None, :]).astype(jnp.bfloat16)


def carry_values(values, block):
    totals = jnp.sum(block.astype(jnp.float32), 0)
    return jnp.dot(values, block, preferred_element_type=jnp.float32) / totals[None, :]


def parent_node(joined, chosen):
    joined_x = joined[:DIM]
    parent_x = jnp.take(joined_x, chosen, axis=1)
    block = kernel_block(joined_x, parent_x)
    parent_up = jnp.dot(spread_weights(joined[DIM:], block), block, preferred_element_type=jnp.float32).astype(jnp.bfloat16)
    return jnp.concatenate([parent_x, parent_up], 0)


def downward_top(sibling, own_x):
    return jnp.dot(sibling[DIM:], kernel_block(sibling[:DIM], own_x), preferred_element_type=jnp.float32).astype(jnp.bfloat16)


def downward_node(sibling, parent_x, parent_down, own_x):
    beside = jnp.dot(sibling[DIM:], kernel_block(sibling[:DIM], own_x), preferred_element_type=jnp.float32)
    above = carry_values(parent_down, kernel_block(parent_x, own_x))
    return (beside + above).astype(jnp.bfloat16)


def near_block(leaves, targets_x, leaf_ids):
    target32 = targets_x.astype(jnp.float32)
    target_norm = jnp.sum(target32 * target32, 1)

    def one_turn(turn, summed):
        source = jnp.take(leaves, leaf_ids[:, turn], axis=0)
        source32 = source[:, :DIM].astype(jnp.float32)
        products = jnp.einsum("bdt,bds->bts", target32, source32, precision=lax.Precision.HIGHEST)
        distance = target_norm[:, :, None] + jnp.sum(source32 * source32, 1)[:, None, :] - 2.0 * products
        weights = jnp.exp(-GAMMA * distance).astype(jnp.bfloat16)
        return summed + jnp.einsum("bts,brs->rbt", weights.astype(jnp.float32), source[:, DIM:].astype(jnp.float32), precision=lax.Precision.HIGHEST)

    start = jnp.zeros((NRHS, targets_x.shape[0], targets_x.shape[2]), jnp.float32)
    return lax.fori_loop(0, leaf_ids.shape[1], one_turn, start)


def reference(points, charges, near_leaves, skel_device, skel_tree):
    nodes = skel_device.shape[0]
    levels = skel_tree.shape[1] + 1
    dev_points = points.shape[1] // nodes
    coords = points.reshape(DIM, nodes, dev_points).transpose(1, 0, 2)
    loads = charges.reshape(NRHS, nodes, dev_points).transpose(1, 0, 2)

    def leaf_up(inputs):
        node_x, node_q, chosen = inputs
        base_x = jnp.take(node_x, chosen, axis=1)
        block = kernel_block(node_x, base_x)
        base_up = jnp.dot(spread_weights(node_q, block), block, preferred_element_type=jnp.float32).astype(jnp.bfloat16)
        return jnp.concatenate([base_x, base_up], 0)

    level_nodes = [lax.map(leaf_up, (coords, loads, skel_device))]
    for height in range(levels - 1):
        current = level_nodes[-1]
        joined = jnp.concatenate([current[0::2], current[1::2]], 2)
        chosen = skel_tree[0::2 ** (height + 1), height]
        level_nodes.append(lax.map(lambda inputs: parent_node(inputs[0], inputs[1]), (joined, chosen)))

    downward = None
    for height in range(levels - 1, -1, -1):
        current = level_nodes[height]
        number = current.shape[0]
        sibling = current.reshape(number // 2, 2, DIM + NRHS, R)[:, ::-1].reshape(number, DIM + NRHS, R)
        if height == levels - 1:
            downward = lax.map(lambda inputs: downward_top(inputs[0], inputs[1][:DIM]), (sibling, current))
        else:
            parent_x = jnp.repeat(level_nodes[height + 1][:, :DIM], 2, axis=0)
            parent_down = jnp.repeat(downward, 2, axis=0)
            downward = lax.map(lambda inputs: downward_node(inputs[0], inputs[1], inputs[2], inputs[3][:DIM]), (sibling, parent_x, parent_down, current))

    base_x = level_nodes[0][:, :DIM]

    def far_field(inputs):
        node_down, node_base, node_x = inputs
        return carry_values(node_down, kernel_block(node_base, node_x))

    far_part = lax.map(far_field, (downward, base_x, coords))

    stacked = jnp.concatenate([points, charges], 0)
    leaves = stacked.reshape(DIM + NRHS, nodes * LEAF_DEV, LEAF).transpose(1, 0, 2)
    id_blocks = near_leaves.reshape(nodes, LEAF_DEV, NNEAR)

    def near_node(inputs):
        node_id, leaf_ids = inputs
        targets = lax.dynamic_slice_in_dim(leaves, (node_id * LEAF_DEV).astype(jnp.int32), LEAF_DEV, 0)
        return near_block(leaves, targets[:, :DIM], leaf_ids).reshape(NRHS, LEAF_DEV * LEAF)

    near_part = lax.map(near_node, (jnp.arange(nodes, dtype=jnp.int32), id_blocks))
    total = near_part + far_part
    return total.transpose(1, 0, 2).reshape(NRHS, nodes * dev_points)
```

```python
import functools

import jax
import jax.numpy as jnp
from jax import lax
from jax.experimental import pallas as pl
from jax.experimental.pallas import tpu as pltpu
from jax.sharding import PartitionSpec as P

DIM = 16
NRHS = 64
DEPTH = 64
GAMMA = 0.125
LOG2E = 1.4426950408889634
MESH = pl.DeviceIdType.MESH
F32 = jnp.float32
BF16 = jnp.bfloat16


def split3(value):
    high = value.astype(BF16).astype(F32)
    rest = value - high
    middle = rest.astype(BF16).astype(F32)
    return [high, middle, rest - middle]


def norms(x32):
    return split3(-(GAMMA * LOG2E) * jnp.sum(x32 * x32, 0, keepdims=True))


def padding(x32):
    return [jnp.zeros((DEPTH - 3 * DIM - 6, x32.shape[1]), F32)]


def row_side(x):
    x32 = x.astype(F32)
    ones = jnp.ones((1, x32.shape[1]), F32)
    parts = split3((2.0 * GAMMA * LOG2E) * x32) + norms(x32) + [ones] * 3 + padding(x32)
    return jnp.concatenate(parts, 0).T.astype(BF16)


def column_side(x):
    x32 = x.astype(F32)
    ones = jnp.ones((1, x32.shape[1]), F32)
    parts = [x32] * 3 + [ones] * 3 + norms(x32) + padding(x32)
    return jnp.concatenate(parts, 0).astype(BF16)


def dot(left, right):
    return jnp.dot(left, right, preferred_element_type=F32)


def dot_nt(left, right):
    return lax.dot_general(left, right, (((1,), (1,)), ((), ())), preferred_element_type=F32)


def gaussian(rows, columns):
    return jnp.exp2(dot(rows, columns)).astype(BF16)


def column_sums(block):
    return jnp.sum(block.astype(F32), 0, keepdims=True)


def picked(source, chosen, first):
    index = lax.broadcasted_iota(jnp.int32, (source.shape[1], chosen.shape[1]), 0) + first
    return dot(source, jnp.where(index == chosen, 1.0, 0.0).astype(BF16))


def kernel(
    inner_levels, outer_levels, near_ref, x_ref, q_ref, device_ref, tree_ref, out_ref,
    xhalo, qhalo, qall, rows, cols, block0, total0, acc, nodes, sibs, blocks, totals, beside,
    halo_send, halo_recv, tree_send, tree_recv,
):
    inner = 1 << inner_levels
    levels = inner_levels + outer_levels
    outer_id, inner_id = lax.axis_index("outer"), lax.axis_index("inner")
    count = inner << outer_levels
    position = outer_id * inner + inner_id
    n = x_ref.shape[1]
    leaf_dev, n_near = near_ref.shape
    leaf = n // leaf_dev
    size = device_ref.shape[1]
    has_left, has_right = position > 0, position < count - 1
    left, right = jnp.maximum(position - 1, 0), jnp.minimum(position + 1, count - 1)
    left_id = (left // inner, left % inner)
    right_id = (right // inner, right % inner)

    bits, partners = [], []
    for k in range(levels):
        if k < inner_levels:
            bit = (inner_id // (1 << k)) % 2
            partners.append((outer_id, inner_id + (1 - 2 * bit) * (1 << k)))
        else:
            step = 1 << (k - inner_levels)
            bit = (outer_id // step) % 2
            partners.append((outer_id + (1 - 2 * bit) * step, inner_id))
        bits.append(bit)

    barrier = pltpu.get_barrier_semaphore()
    for peer in partners:
        pl.semaphore_signal(barrier, inc=1, device_id=peer, device_id_type=MESH)

    @pl.when(has_left)
    def _():
        pl.semaphore_signal(barrier, inc=1, device_id=left_id, device_id_type=MESH)

    @pl.when(has_right)
    def _():
        pl.semaphore_signal(barrier, inc=1, device_id=right_id, device_id_type=MESH)

    chunk = 512
    wide = n // chunk

    def pick(c, total):
        part = pl.ds(pl.multiple_of(c * chunk, chunk), chunk)
        cols[:, part] = column_side(x_ref[:, part])
        return total + picked(x_ref[:, part], device_ref[...], c * chunk)

    base_x = lax.fori_loop(0, wide, pick, jnp.zeros((DIM, size), F32)).astype(BF16)

    sides = (position + count - 1) // count + 1 - (position + 1) // count
    pl.semaphore_wait(barrier, levels + sides)

    def halo(source, target, which, peer):
        return pltpu.make_async_remote_copy(
            src_ref=source, dst_ref=target, send_sem=halo_send.at[which],
            recv_sem=halo_recv.at[which], device_id=peer, device_id_type=MESH,
        )

    rightward = [
        halo(x_ref, xhalo.at[0], 0, right_id),
        halo(q_ref, qhalo.at[0], 1, right_id),
    ]
    leftward = [
        halo(x_ref, xhalo.at[1], 2, left_id),
        halo(q_ref, qhalo.at[1], 3, left_id),
    ]

    @pl.when(has_right)
    def _():
        for copy in rightward:
            copy.start()

    @pl.when(has_left)
    def _():
        for copy in leftward:
            copy.start()

    nodes[0, :DIM, :] = base_x
    base_rows = row_side(base_x)
    acc[...] = jnp.zeros_like(acc)

    def base(c, _):
        part = pl.ds(pl.multiple_of(c * chunk, chunk), chunk)
        block = gaussian(base_rows, cols[:, part])
        total = column_sums(block)
        block0[:, part] = block
        total0[:, part] = 1.0 / total
        weights = (q_ref[:, part].astype(F32) / total).astype(BF16)
        acc[...] += dot_nt(weights, block)
        return 0

    lax.fori_loop(0, wide, base, 0)
    nodes[0, DIM:, :] = acc[...].astype(BF16)

    exchanges = [
        pltpu.make_async_remote_copy(
            src_ref=nodes.at[k], dst_ref=sibs.at[k], send_sem=tree_send.at[k],
            recv_sem=tree_recv.at[k], device_id=partners[k], device_id_type=MESH,
        )
        for k in range(levels)
    ]
    exchanges[0].start()

    def prepare(first, x_source, q_source):
        def one(j, _):
            part = pl.ds(pl.multiple_of(j * leaf, leaf), leaf)
            rows[first + j] = row_side(x_source[:, part])
            qall[first + j] = q_source[:, part]
            return 0

        lax.fori_loop(0, leaf_dev, one, 0)

    def near(b, _):
        part = pl.ds(pl.multiple_of(b * leaf, leaf), leaf)
        columns = cols[:, part]
        weights, loads = [], []
        for turn in range(n_near):
            number = near_ref[b, turn] - (position - 1) * leaf_dev
            number = jnp.minimum(jnp.maximum(number, 0), 3 * leaf_dev - 1)
            weights.append(gaussian(rows[number], columns))
            loads.append(qall[number])
        out_ref[:, part] = dot(jnp.concatenate(loads, 1), jnp.concatenate(weights, 0))
        return 0

    def climb(k):
        own, sib = nodes[k], sibs[k]
        joined_x = jnp.concatenate([own[:DIM], sib[:DIM]], 1)
        shifted = tree_ref[0, k : k + 1, :] + bits[k] * size
        chosen = jnp.where(shifted >= 2 * size, shifted - 2 * size, shifted)
        parent_x = picked(joined_x, chosen, 0).astype(BF16)
        parent_rows = row_side(parent_x)
        up = jnp.zeros((NRHS, size), F32)
        for half in (own, sib):
            block = gaussian(parent_rows, column_side(half[:DIM]))
            total = column_sums(block)
            if half is own:
                blocks[k] = block
                totals[k : k + 1, :] = total
            up = up + dot_nt((half[DIM:].astype(F32) / total).astype(BF16), block)
        nodes[k + 1, :DIM, :] = parent_x
        nodes[k + 1, DIM:, :] = up.astype(BF16)
        exchanges[k + 1].start()

    def across(k):
        own, sib = nodes[k], sibs[k]
        beside[k] = dot(sib[DIM:], gaussian(row_side(sib[:DIM]), column_side(own[:DIM])))

    prepare(leaf_dev, x_ref, q_ref)
    share = max(1, min(2, leaf_dev // levels))
    done = 0
    for k in range(levels):
        exchanges[k].wait_recv()
        if k < levels - 1:
            climb(k)
        across(k)
        if k == 0:
            @pl.when(has_left)
            def _():
                for copy in rightward:
                    copy.wait_recv()

            prepare(0, xhalo.at[0], qhalo.at[0])

            @pl.when(has_right)
            def _():
                for copy in leftward:
                    copy.wait_recv()

            prepare(2 * leaf_dev, xhalo.at[1], qhalo.at[1])
        ahead = min(leaf_dev, done + share) if k < levels - 1 else leaf_dev
        if ahead > done:
            lax.fori_loop(done, ahead, near, 0)
        done = ahead

    down = beside[levels - 1].astype(BF16)
    for k in range(levels - 2, -1, -1):
        down = (beside[k] + dot(down, blocks[k]) / totals[k : k + 1, :]).astype(BF16)

    def far(c, _):
        part = pl.ds(pl.multiple_of(c * chunk, chunk), chunk)
        out_ref[:, part] += dot(down, block0[:, part]) * total0[:, part]
        return 0

    lax.fori_loop(0, wide, far, 0)

    for copy in exchanges:
        copy.wait_send()

    @pl.when(has_right)
    def _():
        for copy in rightward:
            copy.wait_send()

    @pl.when(has_left)
    def _():
        for copy in leftward:
            copy.wait_send()


def body(points, charges, near_leaves, skel_device, skel_tree):
    inner_levels = lax.axis_size("inner").bit_length() - 1
    outer_levels = lax.axis_size("outer").bit_length() - 1
    levels = inner_levels + outer_levels
    n, size = points.shape[1], skel_device.shape[1]
    leaf_dev = near_leaves.shape[0]
    leaf = n // leaf_dev
    vmem = pl.BlockSpec(memory_space=pltpu.VMEM)
    node = (levels, DIM + NRHS, size)
    return pl.pallas_call(
        functools.partial(kernel, inner_levels, outer_levels),
        out_shape=jax.ShapeDtypeStruct((NRHS, n), F32),
        in_specs=[pl.BlockSpec(memory_space=pltpu.SMEM)] + [vmem] * 4,
        out_specs=vmem,
        scratch_shapes=[
            pltpu.VMEM((2, DIM, n), BF16),
            pltpu.VMEM((2, NRHS, n), BF16),
            pltpu.VMEM((3 * leaf_dev, NRHS, leaf), BF16),
            pltpu.VMEM((3 * leaf_dev, leaf, DEPTH), BF16),
            pltpu.VMEM((DEPTH, n), BF16),
            pltpu.VMEM((size, n), BF16),
            pltpu.VMEM((1, n), F32),
            pltpu.VMEM((NRHS, size), F32),
            pltpu.VMEM(node, BF16),
            pltpu.VMEM(node, BF16),
            pltpu.VMEM((levels, size, size), BF16),
            pltpu.VMEM((levels, size), F32),
            pltpu.VMEM((levels, NRHS, size), F32),
            pltpu.SemaphoreType.DMA((4,)),
            pltpu.SemaphoreType.DMA((4,)),
            pltpu.SemaphoreType.DMA((levels,)),
            pltpu.SemaphoreType.DMA((levels,)),
        ],
        compiler_params=pltpu.CompilerParams(
            collective_id=0, has_side_effects=True, vmem_limit_bytes=50 << 20
        ),
        name="skeleton_matvec",
    )(near_leaves, points, charges, skel_device, skel_tree)


def solution(mesh):
    return jax.shard_map(
        body,
        mesh=mesh,
        in_specs=(
            P(None, ("outer", "inner")),
            P(None, ("outer", "inner")),
            P(("outer", "inner"), None),
            P(("outer", "inner"), None),
            P(("outer", "inner"), None, None),
        ),
        out_specs=P(None, ("outer", "inner")),
        check_vma=False,
    )
```

```python
import functools

import jax
import jax.numpy as jnp
from jax import lax
from jax.experimental import pallas as pl
from jax.experimental.pallas import tpu as pltpu
from jax.sharding import PartitionSpec as P

DIM = 16
NRHS = 64
DEPTH = 64
GAMMA = 0.125
LOG2E = 1.4426950408889634
MESH = pl.DeviceIdType.MESH
F32 = jnp.float32
BF16 = jnp.bfloat16


def split3(value):
    high = value.astype(BF16).astype(F32)
    rest = value - high
    middle = rest.astype(BF16).astype(F32)
    return [high, middle, rest - middle]


def norms(x32):
    return split3(-(GAMMA * LOG2E) * jnp.sum(x32 * x32, 0, keepdims=True))


def padding(x32):
    return [jnp.zeros((DEPTH - 3 * DIM - 6, x32.shape[1]), F32)]


def row_side(x):
    x32 = x.astype(F32)
    ones = jnp.ones((1, x32.shape[1]), F32)
    parts = split3((2.0 * GAMMA * LOG2E) * x32) + norms(x32) + [ones] * 3 + padding(x32)
    return jnp.concatenate(parts, 0).T.astype(BF16)


def column_side(x):
    x32 = x.astype(F32)
    ones = jnp.ones((1, x32.shape[1]), F32)
    parts = [x32] * 3 + [ones] * 3 + norms(x32) + padding(x32)
    return jnp.concatenate(parts, 0).astype(BF16)


def dot(left, right):
    return jnp.dot(left, right, preferred_element_type=F32)


def dot_nt(left, right):
    return lax.dot_general(left, right, (((1,), (1,)), ((), ())), preferred_element_type=F32)


def gaussian(rows, columns):
    return jnp.exp2(dot(rows, columns)).astype(BF16)


def column_sums(block):
    return jnp.sum(block.astype(F32), 0, keepdims=True)


def picked(source, chosen, first):
    index = lax.broadcasted_iota(jnp.int32, (source.shape[1], chosen.shape[1]), 0) + first
    return dot(source, jnp.where(index == chosen, 1.0, 0.0).astype(BF16))


def kernel(
    inner_levels, outer_levels, near_hbm, x_hbm, q_hbm, device_hbm, tree_hbm, out_ref,
    near_ref, x_ref, q_ref, device_ref, tree_ref, xhalo, qhalo, qall, rows, cols, block0, total0, acc, nodes, sibs, blocks, totals, beside,
    halo_send, halo_recv, tree_send, tree_recv, local_sem,
):
    inner = 1 << inner_levels
    levels = inner_levels + outer_levels
    outer_id, inner_id = lax.axis_index("outer"), lax.axis_index("inner")
    count = inner << outer_levels
    position = outer_id * inner + inner_id
    n = x_ref.shape[1]
    leaf_dev, n_near = near_ref.shape
    leaf = n // leaf_dev
    size = device_ref.shape[1]
    has_left, has_right = position > 0, position < count - 1
    left, right = jnp.maximum(position - 1, 0), jnp.minimum(position + 1, count - 1)
    left_id = (left // inner, left % inner)
    right_id = (right // inner, right % inner)

    bits, partners = [], []
    for k in range(levels):
        if k < inner_levels:
            bit = (inner_id // (1 << k)) % 2
            partners.append((outer_id, inner_id + (1 - 2 * bit) * (1 << k)))
        else:
            step = 1 << (k - inner_levels)
            bit = (outer_id // step) % 2
            partners.append((outer_id + (1 - 2 * bit) * step, inner_id))
        bits.append(bit)

    sources = (x_hbm, device_hbm, q_hbm, tree_hbm, near_hbm)
    targets = (x_ref, device_ref, q_ref, tree_ref, near_ref)
    loads = [
        pltpu.make_async_copy(source, target, local_sem.at[i])
        for i, (source, target) in enumerate(zip(sources, targets))
    ]
    for load in loads:
        load.start()

    barrier = pltpu.get_barrier_semaphore()
    for peer in partners:
        pl.semaphore_signal(barrier, inc=1, device_id=peer, device_id_type=MESH)

    @pl.when(has_left)
    def _():
        pl.semaphore_signal(barrier, inc=1, device_id=left_id, device_id_type=MESH)

    @pl.when(has_right)
    def _():
        pl.semaphore_signal(barrier, inc=1, device_id=right_id, device_id_type=MESH)

    chunk = 512
    wide = n // chunk

    def pick(c, total):
        part = pl.ds(pl.multiple_of(c * chunk, chunk), chunk)
        cols[:, part] = column_side(x_ref[:, part])
        return total + picked(x_ref[:, part], device_ref[...], c * chunk)

    loads[0].wait()
    loads[1].wait()
    base_x = lax.fori_loop(0, wide, pick, jnp.zeros((DIM, size), F32), unroll=4).astype(BF16)

    beside_us = (position + count - 1) // count + 1 - (position + 1) // count
    pl.semaphore_wait(barrier, levels + beside_us)

    def halo(source, target, which, peer):
        return pltpu.make_async_remote_copy(
            src_ref=source, dst_ref=target, send_sem=halo_send.at[which],
            recv_sem=halo_recv.at[which], device_id=peer, device_id_type=MESH,
        )

    rightward = [
        halo(x_hbm, xhalo.at[0], 0, right_id),
        halo(q_hbm, qhalo.at[0], 1, right_id),
    ]
    leftward = [
        halo(x_hbm, xhalo.at[1], 2, left_id),
        halo(q_hbm, qhalo.at[1], 3, left_id),
    ]

    @pl.when(has_right)
    def _():
        for copy in rightward:
            copy.start()

    @pl.when(has_left)
    def _():
        for copy in leftward:
            copy.start()

    nodes[0, :DIM, :] = base_x
    base_rows = row_side(base_x)
    acc[...] = jnp.zeros_like(acc)

    def base(c, _):
        part = pl.ds(pl.multiple_of(c * chunk, chunk), chunk)
        block = gaussian(base_rows, cols[:, part])
        total = column_sums(block)
        block0[:, part] = block
        inverse = 1.0 / total
        total0[:, part] = inverse
        weights = (q_ref[:, part].astype(F32) * inverse).astype(BF16)
        acc[...] += dot_nt(weights, block)
        return 0

    for load in loads[2:]:
        load.wait()
    lax.fori_loop(0, wide, base, 0, unroll=2)
    nodes[0, DIM:, :] = acc[...].astype(BF16)

    exchanges = [
        pltpu.make_async_remote_copy(
            src_ref=nodes.at[k], dst_ref=sibs.at[k], send_sem=tree_send.at[k],
            recv_sem=tree_recv.at[k], device_id=partners[k], device_id_type=MESH,
        )
        for k in range(levels)
    ]
    exchanges[0].start()

    def prepare(first, x_source, q_source):
        def one(j, _):
            part = pl.ds(pl.multiple_of(j * leaf, leaf), leaf)
            rows[first + j] = row_side(x_source[:, part])
            qall[first + j] = q_source[:, part]
            return 0

        lax.fori_loop(0, leaf_dev, one, 0, unroll=8)

    def near(b, _):
        part = pl.ds(pl.multiple_of(b * leaf, leaf), leaf)
        columns = cols[:, part]
        weights, sides = [], []
        for turn in range(n_near):
            number = near_ref[b, turn] - (position - 1) * leaf_dev
            number = jnp.minimum(jnp.maximum(number, 0), 3 * leaf_dev - 1)
            weights.append(gaussian(rows[number], columns))
            sides.append(qall[number])
        out_ref[:, part] = dot(jnp.concatenate(sides, 1), jnp.concatenate(weights, 0))
        return 0

    def climb(k):
        own, sib = nodes[k], sibs[k]
        joined_x = jnp.concatenate([own[:DIM], sib[:DIM]], 1)
        shifted = tree_ref[0, k : k + 1, :] + bits[k] * size
        chosen = jnp.where(shifted >= 2 * size, shifted - 2 * size, shifted)
        parent_x = picked(joined_x, chosen, 0).astype(BF16)
        parent_rows = row_side(parent_x)
        up = jnp.zeros((NRHS, size), F32)
        for half in (own, sib):
            block = gaussian(parent_rows, column_side(half[:DIM]))
            inverse = 1.0 / column_sums(block)
            if half is own:
                blocks[k] = block
                totals[k : k + 1, :] = inverse
            up = up + dot_nt((half[DIM:].astype(F32) * inverse).astype(BF16), block)
        nodes[k + 1, :DIM, :] = parent_x
        nodes[k + 1, DIM:, :] = up.astype(BF16)
        exchanges[k + 1].start()

    def across(k):
        own, sib = nodes[k], sibs[k]
        beside[k] = dot(sib[DIM:], gaussian(row_side(sib[:DIM]), column_side(own[:DIM])))

    prepare(leaf_dev, x_ref, q_ref)
    share = max(1, min(2, leaf_dev // levels))
    done = 0
    for k in range(levels):
        exchanges[k].wait_recv()
        if k < levels - 1:
            climb(k)
        across(k)
        if k == 0:

            @pl.when(has_left)
            def _():
                for copy in rightward:
                    copy.wait_recv()

            prepare(0, xhalo.at[0], qhalo.at[0])

            @pl.when(has_right)
            def _():
                for copy in leftward:
                    copy.wait_recv()

            prepare(2 * leaf_dev, xhalo.at[1], qhalo.at[1])
        ahead = min(leaf_dev, done + share) if k < levels - 1 else leaf_dev
        if ahead > done:
            lax.fori_loop(done, ahead, near, 0)
        done = ahead

    down = beside[levels - 1].astype(BF16)
    for k in range(levels - 2, -1, -1):
        down = (beside[k] + dot(down, blocks[k]) * totals[k : k + 1, :]).astype(BF16)

    def far(c, _):
        part = pl.ds(pl.multiple_of(c * chunk, chunk), chunk)
        out_ref[:, part] += dot(down, block0[:, part]) * total0[:, part]
        return 0

    lax.fori_loop(0, wide, far, 0, unroll=2)

    for copy in exchanges:
        copy.wait_send()

    @pl.when(has_right)
    def _():
        for copy in rightward:
            copy.wait_send()

    @pl.when(has_left)
    def _():
        for copy in leftward:
            copy.wait_send()


def body(points, charges, near_leaves, skel_device, skel_tree):
    inner_levels = lax.axis_size("inner").bit_length() - 1
    outer_levels = lax.axis_size("outer").bit_length() - 1
    levels = inner_levels + outer_levels
    n, size = points.shape[1], skel_device.shape[1]
    leaf_dev = near_leaves.shape[0]
    leaf = n // leaf_dev
    vmem = pl.BlockSpec(memory_space=pltpu.VMEM)
    node = (levels, DIM + NRHS, size)
    return pl.pallas_call(
        functools.partial(kernel, inner_levels, outer_levels),
        out_shape=jax.ShapeDtypeStruct((NRHS, n), F32),
        in_specs=[pl.BlockSpec(memory_space=pltpu.HBM)] * 5,
        out_specs=vmem,
        scratch_shapes=[
            pltpu.SMEM(near_leaves.shape, jnp.int32),
            pltpu.VMEM(points.shape, BF16),
            pltpu.VMEM(charges.shape, BF16),
            pltpu.VMEM(skel_device.shape, jnp.int32),
            pltpu.VMEM(skel_tree.shape, jnp.int32),
            pltpu.VMEM((2, DIM, n), BF16),
            pltpu.VMEM((2, NRHS, n), BF16),
            pltpu.VMEM((3 * leaf_dev, NRHS, leaf), BF16),
            pltpu.VMEM((3 * leaf_dev, leaf, DEPTH), BF16),
            pltpu.VMEM((DEPTH, n), BF16),
            pltpu.VMEM((size, n), BF16),
            pltpu.VMEM((1, n), F32),
            pltpu.VMEM((NRHS, size), F32),
            pltpu.VMEM(node, BF16),
            pltpu.VMEM(node, BF16),
            pltpu.VMEM((levels, size, size), BF16),
            pltpu.VMEM((levels, size), F32),
            pltpu.VMEM((levels, NRHS, size), F32),
            pltpu.SemaphoreType.DMA((4,)),
            pltpu.SemaphoreType.DMA((4,)),
            pltpu.SemaphoreType.DMA((levels,)),
            pltpu.SemaphoreType.DMA((levels,)),
            pltpu.SemaphoreType.DMA((5,)),
        ],
        compiler_params=pltpu.CompilerParams(
            collective_id=0, has_side_effects=True, vmem_limit_bytes=50 << 20
        ),
        name="skeleton_matvec",
    )(near_leaves, points, charges, skel_device, skel_tree)


def solution(mesh):
    return jax.shard_map(
        body,
        mesh=mesh,
        in_specs=(
            P(None, ("outer", "inner")),
            P(None, ("outer", "inner")),
            P(("outer", "inner"), None),
            P(("outer", "inner"), None),
            P(("outer", "inner"), None, None),
        ),
        out_specs=P(None, ("outer", "inner")),
        check_vma=False,
    )
```
